32 devices in a mesh: expert: 8 (over y, x, core), dp: 4 (over z).
Axes of the slice: x: 2, y: 2, z: 4, core: 2. Of those that a mesh axis runs over, the one named last changes fastest.
Arguments:
- tokens: bfloat16 [512, 2048], P(('expert', 'dp')), may hold values from -6 to 6
- out_grad: bfloat16 [512, 2048], P(('expert', 'dp')), may hold values from -6 to 6
- routes: int32 [512, 8], P(('expert', 'dp')), may hold values from 0 to 15, all different within a row; in each aligned block of 16 rows (0 to 15, 16 to 31, ...) at most 16 rows name the same one
- route_gates: float32 [512, 8], P(('expert', 'dp')), may hold values from 0.05 to 0.5
- w_gate: bfloat16 [16, 2048, 384], P('expert'), may hold values from -0.125 to 0.125
- w_up: bfloat16 [16, 2048, 384], P('expert'), may hold values from -0.125 to 0.125
- w_down: bfloat16 [16, 384, 2048], P('expert'), may hold values from -0.3125 to 0.3125
Outputs:
- token_grad: bfloat16 [512, 2048], P(('expert', 'dp'))
- down_grad: float32 [384, 16, 2048], P('dp', 'expert')
The draws below stay inside these ranges and needn't reach their ends.
Inputs may be any that keep to these rules, and one draw needn't show every extreme that they name: `routes`: each row names 8 different experts. Among the 16 tokens of one device no expert is named more than 16 times, a bound that some block reaches.
All inputs are finite; a program needn't handle non-finite values.
Results may differ from the reference program's by a relative error of at most 0.014.
Values may be sent and summed in bfloat16 or wider, within the bound.
A program may use at most 64 MiB of HBM per device.

```python
import math
import jax
import jax.numpy as jnp
import numpy as np
from jax import lax

D = 2048
TOP = 8
FF = 384
TOK_DEV = 16
EXPERTS = 16
CAP = 16
TOKENS = 512
N_EXPERT = 8
N_DP = 4


def block_levels(rng, dims, split, least, high):
    def one(dim, parts):
        steps = jax.random.uniform(jax.random.fold_in(jax.random.fold_in(rng, 6), dim), (parts,), jnp.float32, least / len(split), high / len(split))
        return jnp.repeat(jnp.exp(steps), dims[dim] // parts).reshape((-1,) + (1,) * (len(dims) - dim - 1))

    level = one(*split[0])
    for cut in split[1:]:
        level = level * one(*cut)
    return level


def routed_block(own_key, own, number, rows, amount, top, most, slope):
    sequence = jax.random.permutation(own_key, amount)
    packed, common = load_shares(amount, rows * top, most, slope, True), load_shares(amount, rows * top, most, slope, False)
    places = jnp.arange(amount)

    def named(tallies, offset_by):
        used = int((tallies > 0).sum())
        fixed = max(1, used // 4)
        passed = fixed + (places - fixed + offset_by * (used - fixed)) % max(1, amount - fixed)
        return jnp.zeros((amount,), jnp.int32).at[sequence[jnp.where(places < fixed, places, passed)]].set(jnp.asarray(tallies, jnp.int32))

    tallies = jnp.where(number % 4 == 0, named(packed, number // 4), named(common, number - number // 4 - 1))
    mixed = jax.random.permutation(jax.random.fold_in(own, 3), amount)
    source_of, taker = mixed[0:amount // 2 * 2:2], mixed[1:amount // 2 * 2:2]
    room = jnp.minimum(tallies[source_of] - 1, most - tallies[taker]) // 2
    room = jnp.where((source_of == sequence[0]) | (taker == sequence[0]) | (tallies[taker] == 0), 0, jnp.maximum(room, 0))
    passed = jax.random.randint(jax.random.fold_in(own, 4), (amount // 2,), 0, 1 << 20) % (room + 1)
    tallies = tallies.at[source_of].add(-passed).at[taker].add(passed)
    members = jnp.searchsorted(jnp.cumsum(tallies), jnp.arange(rows * top), side="right").astype(jnp.int32)
    grid = members.reshape(top, rows).T
    grid = grid[jax.random.permutation(jax.random.fold_in(own, 1), rows)]
    offset_by = jax.random.randint(jax.random.fold_in(own, 2), (rows, 1), 0, top)
    return jnp.take_along_axis(grid, (jnp.arange(top)[None, :] + offset_by) % top, axis=1)


def load_shares(count, total, most, slope, full):
    portions = [(1 << 20) // math.isqrt(rank ** slope) + 1 for rank in range(1, count + 1)]
    largest = most if full else min(most, max(-(-total // count), total * portions[0] // sum(portions)))
    least = 1 if total - largest >= count - 1 else 0
    counts, surplus = [largest] + [least] * (count - 1), total - largest - least * (count - 1)
    while surplus > 0:
        free = [i for i in range(1, count) if counts[i] < largest] or [i for i in range(1, count) if counts[i] < most]
        pool, remaining = sum([portions[i] for i in free]), surplus
        for i in free:
            extra = min(most - counts[i], max(1, remaining * portions[i] // pool), surplus)
            counts[i] = counts[i] + extra
            surplus = surplus - extra
    return np.array(counts)


def gaussian(rng, dims, scale, most, pieces=(), kind=jnp.bfloat16):
    values = scale * jax.random.normal(rng, dims, jnp.float32)
    if pieces:
        values = values * block_levels(rng, dims, pieces, -0.22, 0.18)
    return jnp.clip(values, -most, most).astype(kind)


def setup_inputs(seed: int = 0) -> dict:
    arg_keys = jax.random.split(jax.random.key(seed), 8)
    tokens = gaussian(arg_keys[0], (TOKENS, D), 1.0, 6.0, ((0, 32),))
    out_grad = gaussian(arg_keys[1], (TOKENS, D), 1.0, 6.0, ((0, 32),))
    routes_keys = jax.random.split(jax.random.fold_in(arg_keys[2], 1), TOKENS // TOK_DEV)
    routes_turns = jax.random.permutation(jax.random.fold_in(arg_keys[2], 3), TOKENS // TOK_DEV)
    routes = jax.vmap(lambda own, number: routed_block(jax.random.fold_in(arg_keys[2], 2), own, number, TOK_DEV, EXPERTS, TOP, CAP, 2))(routes_keys, routes_turns).reshape((TOKENS, TOP))
    route_gates = jnp.clip(jnp.exp(math.log(0.5) - 2.3025851 * jax.random.uniform(arg_keys[3], (TOKENS, TOP), jnp.float32) ** block_levels(arg_keys[3], (TOKENS, TOP), ((0, 32),), -0.2, 0.2)), 0.05, 0.5)
    w_gate = gaussian(arg_keys[4], (EXPERTS, D, FF), D ** -0.5, 0.125, ((0, 8),))
    w_up = gaussian(arg_keys[5], (EXPERTS, D, FF), D ** -0.5, 0.125, ((0, 8),))
    w_down = gaussian(arg_keys[6], (EXPERTS, FF, D), FF ** -0.5, 0.3125, ((0, 8),))
    return {"tokens": tokens, "out_grad": out_grad, "routes": routes, "route_gates": route_gates, "w_gate": w_gate, "w_up": w_up, "w_down": w_down}


def reference(tokens, out_grad, routes, route_gates, w_gate, w_up, w_down):
    span = TOK_DEV * TOP
    limit = N_EXPERT * span
    most_rows = N_EXPERT * CAP
    group_routes = routes.reshape(N_EXPERT, N_DP, span).transpose(1, 0, 2).reshape(N_DP, limit)
    dp_iota = jnp.arange(N_DP, dtype=jnp.int32)

    def expert_pass(carry, inputs):
        expert_id, gate_mat, up_mat, down_mat = inputs
        hits = group_routes == expert_id
        positions = jax.vmap(lambda m: jnp.nonzero(m, size=most_rows, fill_value=limit)[0])(hits).astype(jnp.int32)
        valid = positions < limit
        safe = jnp.where(valid, positions, 0).astype(jnp.int32)
        owner = safe // span
        local = (safe // TOP) % TOK_DEV
        choice_k = safe % TOP
        token_index = ((owner * N_DP + dp_iota[:, None]) * TOK_DEV + local).astype(jnp.int32)
        x_rows = jnp.where(valid[..., None], tokens[token_index], jnp.zeros((), tokens.dtype))
        gain = jnp.where(valid, route_gates[token_index, choice_k], 0.0)
        dy_rows = (gain[..., None] * out_grad[token_index].astype(jnp.float32)).astype(jnp.bfloat16)
        x32 = x_rows.astype(jnp.float32)
        dy32 = dy_rows.astype(jnp.float32)
        gate_pre = jnp.einsum('pmd,df->pmf', x32, gate_mat.astype(jnp.float32))
        up_pre = jnp.einsum('pmd,df->pmf', x32, up_mat.astype(jnp.float32))
        sigmoid_gate = jax.nn.sigmoid(gate_pre)
        silu_gate = gate_pre * sigmoid_gate
        hidden = (silu_gate * up_pre).astype(jnp.bfloat16)
        hidden_grad = jnp.einsum('pmd,fd->pmf', dy32, down_mat.astype(jnp.float32))
        gate_grad = (hidden_grad * up_pre * (sigmoid_gate + gate_pre * sigmoid_gate * (1.0 - sigmoid_gate))).astype(jnp.bfloat16)
        up_grad = (hidden_grad * silu_gate).astype(jnp.bfloat16)
        row_grad = (jnp.einsum('pmf,df->pmd', gate_grad.astype(jnp.float32), gate_mat.astype(jnp.float32))
                    + jnp.einsum('pmf,df->pmd', up_grad.astype(jnp.float32), up_mat.astype(jnp.float32))).astype(jnp.bfloat16)
        part = jnp.einsum('pmf,pmd->pfd', hidden.astype(jnp.float32), dy32).astype(jnp.bfloat16)
        part = lax.optimization_barrier(part)
        down_part = jnp.sum(part.astype(jnp.float32), axis=0)
        added = jnp.where(valid[..., None], row_grad.astype(jnp.float32), 0.0)
        carry = carry.at[token_index.reshape(-1)].add(added.reshape(-1, D))
        return carry, down_part

    start_grad = jnp.zeros((TOKENS, D), jnp.float32)
    expert_ids = jnp.arange(EXPERTS, dtype=jnp.int32)
    token_grad, downs = lax.scan(expert_pass, start_grad, (expert_ids, w_gate, w_up, w_down))
    return token_grad.astype(jnp.bfloat16), jnp.transpose(downs, (1, 0, 2))
```

```python
import functools

import jax
import jax.numpy as jnp
from jax import lax
from jax.experimental import pallas as pl
from jax.experimental.pallas import tpu as pltpu
from jax.sharding import PartitionSpec as P

VMEM_BUDGET = 44 << 20
NT = (((1,), (1,)), ((), ()))


def gate_up(arrived, w_gate, w_up):
    gate_pre = jnp.einsum("erd,edf->erf", arrived, w_gate, preferred_element_type=jnp.float32)
    up_pre = jnp.einsum("erd,edf->erf", arrived, w_up, preferred_element_type=jnp.float32)
    return (gate_pre, up_pre)


def collective_shards(tokens, out_grad, routes, route_gates, w_gate, w_up, w_down):
    tok_count, model_width = tokens.shape
    top_count = routes.shape[1]
    local_experts = w_gate.shape[0]
    groups = lax.axis_size("expert")
    experts = local_experts * groups
    slot_count = 2 * tok_count * top_count // experts
    flat_routes = routes.reshape(-1)
    onehot = (flat_routes[:, None] == jnp.arange(experts, dtype=jnp.int32)[None, :]).astype(
        jnp.int32
    )
    slot_rank = jnp.sum(onehot * (jnp.cumsum(onehot, axis=0) - onehot), axis=1)
    slot_index = flat_routes * slot_count + slot_rank
    placement = slot_index[None, :] == jnp.arange(experts * slot_count, dtype=jnp.int32)[:, None]
    route_place = placement.astype(jnp.bfloat16)
    token_place = jnp.sum(
        placement.reshape(experts * slot_count, tok_count, top_count).astype(jnp.float32), axis=2
    ).astype(jnp.bfloat16)
    send_inputs = (
        jnp.dot(token_place, tokens, preferred_element_type=jnp.float32)
        .astype(jnp.bfloat16)
        .reshape(experts, slot_count, model_width)
    )
    scaled = (
        (route_gates[:, :, None] * out_grad[:, None, :].astype(jnp.float32))
        .astype(jnp.bfloat16)
        .reshape(tok_count * top_count, model_width)
    )
    send_grads = (
        jnp.dot(route_place, scaled, preferred_element_type=jnp.float32)
        .astype(jnp.bfloat16)
        .reshape(experts, slot_count, model_width)
    )
    arrived, arrived_grad = (
        lax.all_to_all(send_inputs, "expert", split_axis=0, concat_axis=1, tiled=True),
        lax.all_to_all(send_grads, "expert", split_axis=0, concat_axis=1, tiled=True),
    )
    gate_pre, up_pre = gate_up(arrived, w_gate, w_up)
    sigmoid_gate = jax.nn.sigmoid(gate_pre)
    silu_gate = gate_pre * sigmoid_gate
    hidden = (silu_gate * up_pre).astype(jnp.bfloat16)
    hidden_grad = jnp.einsum(
        "erd,efd->erf", arrived_grad, w_down, preferred_element_type=jnp.float32
    )
    gate_grad = (
        hidden_grad * up_pre * (sigmoid_gate + gate_pre * sigmoid_gate * (1.0 - sigmoid_gate))
    ).astype(jnp.bfloat16)
    up_grad = (hidden_grad * silu_gate).astype(jnp.bfloat16)
    row_grads = (
        jnp.einsum("erf,edf->erd", gate_grad, w_gate, preferred_element_type=jnp.float32)
        + jnp.einsum("erf,edf->erd", up_grad, w_up, preferred_element_type=jnp.float32)
    ).astype(jnp.bfloat16)
    returned = lax.all_to_all(row_grads, "expert", split_axis=1, concat_axis=0, tiled=True)
    token_grad = lax.dot_general(
        token_place,
        returned.reshape(experts * slot_count, model_width),
        (((0,), (0,)), ((), ())),
        preferred_element_type=jnp.float32,
    ).astype(jnp.bfloat16)
    hidden_units = hidden.shape[2]
    share_rows = hidden_units // lax.axis_size("dp")
    partial_grad = jnp.einsum(
        "erf,erd->fed", hidden, arrived_grad, preferred_element_type=jnp.float32
    ).astype(jnp.bfloat16)
    total_grad = lax.psum(partial_grad, "dp").astype(jnp.float32)
    first_row = lax.axis_index("dp") * share_rows
    down_grad = lax.dynamic_slice_in_dim(total_grad, first_row, share_rows, 0)
    return (token_grad, down_grad)


def flip(index, bits):
    out, step = index, 1
    while step <= bits:
        if bits & step:
            out = out + step * (1 - 2 * ((index // step) % 2))
        step *= 2
    return out


def copy_keys(chips, planes, local_experts, parts):
    keys = []
    for name in ("x", "r", "g"):
        keys += [(name, d) for d in range(1, chips)] + [(name + "c", d) for d in range(chips)]
    keys += [("z", k) for k in range(1, planes)]
    keys += [("d", k, d) for k in range(planes) for d in range(1, chips)]
    keys += [("dc", k, d) for k in range(planes) for d in range(chips)]
    keys += [("h", k, e) for k in range(1, planes) for e in range(local_experts)]
    keys += [("p", j) for j in range(parts)]
    keys += [("t", j, d) for j in range(parts) for d in range(1, chips)]
    return {key: i for i, key in enumerate(keys)}


def fused_kernel(
    chips, planes, parts, tok, dy, rt, gt, wg, wu, wd, token_out, down_out,
    xb, db, rb, gb, wgv, wuv, wdv, gates, ups, hid_out, hid_in, grads_g, grads_u,
    keep, pair_out, pair_in, ret_out, ret_in, lsem, ssem, rsem,
):
    local_experts, model_width, hidden_units = wg.shape
    rows = tok.shape[0]
    count = 2 * chips * rows
    share = hidden_units // planes
    width = model_width // parts
    me, plane = lax.axis_index("expert"), lax.axis_index("dp")
    chip, core = me // 2, me % 2
    partner = {"expert": chip * 2 + 1 - core, "dp": plane}
    across = [{"expert": flip(chip, d) * 2 + core, "dp": plane} for d in range(chips)]
    above = [{"expert": me, "dp": flip(plane, k)} for k in range(planes)]
    keys = copy_keys(chips, planes, local_experts, parts)

    local = []

    def load(src, dst):
        c = pltpu.make_async_copy(src, dst, lsem.at[len(local)])
        c.start()
        local.append(c)
        return c

    own = [load(tok, xb.at[0]), load(rt, rb.at[0]), load(gt, gb.at[0]), load(dy, db.at[0, 0])]
    gate_up_loads = [(load(wg.at[e], wgv.at[e]), load(wu.at[e], wuv.at[e])) for e in range(local_experts)]
    down_loads = [load(wd.at[e], wdv.at[e]) for e in range(local_experts)]

    def remote(key, src, dst, target):
        i = keys[key]
        return pltpu.make_async_remote_copy(
            src_ref=src, dst_ref=dst, send_sem=ssem.at[i], recv_sem=rsem.at[i],
            device_id=target, device_id_type=pl.DeviceIdType.MESH,
        )

    copies = {}
    for name, src, buf in (("x", tok, xb), ("r", rt, rb), ("g", gt, gb)):
        for d in range(chips):
            if d:
                copies[name, d] = remote((name, d), src, buf.at[2 * d], across[d])
            copies[name + "c", d] = remote(
                (name + "c", d), buf.at[2 * d] if d else src, buf.at[2 * d + 1], partner
            )
    for k in range(planes):
        if k:
            copies["z", k] = remote(("z", k), dy, db.at[k, 0], above[k])
        block = db.at[k, 0] if k else dy
        for d in range(chips):
            if d:
                copies["d", k, d] = remote(("d", k, d), block, db.at[k, 2 * d], across[d])
            copies["dc", k, d] = remote(
                ("dc", k, d), db.at[k, 2 * d] if d else block, db.at[k, 2 * d + 1], partner
            )
    for k in range(1, planes):
        first = pl.multiple_of(flip(plane, k) * share, 16)
        for e in range(local_experts):
            copies["h", k, e] = remote(
                ("h", k, e), hid_out.at[e, pl.ds(first, share)], hid_in.at[k, e], above[k]
            )
    for j in range(parts):
        copies["p", j] = remote(("p", j), pair_out.at[j], pair_in.at[j], partner)
        for d in range(1, chips):
            copies["t", j, d] = remote(("t", j, d), ret_out.at[j, d], ret_in.at[j, d], across[d])

    barrier = pltpu.get_barrier_semaphore()
    targets = [partner] + across[1:] + above[1:]
    for target in targets:
        pl.semaphore_signal(barrier, inc=1, device_id=target, device_id_type=pl.DeviceIdType.MESH)
    pl.semaphore_wait(barrier, len(targets))

    for name in ("x", "r", "g"):
        for d in range(1, chips):
            copies[name, d].start()
    for k in range(planes - 1, 0, -1):
        copies["z", k].start()
    for d in range(1, chips):
        copies["d", 0, d].start()
    for name in ("x", "r", "g"):
        copies[name + "c", 0].start()
    copies["dc", 0, 0].start()

    for d in range(1, chips):
        for name in ("x", "r", "g"):
            copies[name, d].wait_recv()
            copies[name + "c", d].start()
    for c in own:
        c.wait()
    for d in range(chips):
        for name in ("x", "r", "g"):
            copies[name + "c", d].wait_recv()

    x = xb[...].reshape(count, model_width)
    for e in range(local_experts):
        for c in gate_up_loads[e]:
            c.wait()
        gates[e] = jnp.dot(x, wgv[e], preferred_element_type=jnp.float32)
        ups[e] = jnp.dot(x, wuv[e], preferred_element_type=jnp.float32)
        if e == 0:
            for d in range(1, chips):
                copies["d", 0, d].wait_recv()
                copies["dc", 0, d].start()
    for k in range(1, planes):
        copies["z", k].wait_recv()
        for d in range(1, chips):
            copies["d", k, d].start()
        copies["dc", k, 0].start()
    for d in range(chips):
        copies["dc", 0, d].wait_recv()

    named = rb[...].reshape(count, rb.shape[2])
    given = gb[...].reshape(count, gb.shape[2])
    grad_rows = db[0].reshape(count, model_width)
    for e in range(local_experts):
        down_loads[e].wait()
        gain = jnp.sum(
            jnp.where(named == me * local_experts + e, given, 0.0), axis=1, keepdims=True
        )
        hidden_grad = gain * lax.dot_general(
            grad_rows, wdv[e], NT, preferred_element_type=jnp.float32
        )
        gate_pre, up_pre = gates[e], ups[e]
        s = jax.nn.sigmoid(gate_pre)
        silu = gate_pre * s
        hid_out[e] = (silu * up_pre * gain).T.astype(jnp.bfloat16)
        grads_g[e] = (hidden_grad * up_pre * (s + gate_pre * s * (1.0 - s))).astype(jnp.bfloat16)
        grads_u[e] = (hidden_grad * silu).astype(jnp.bfloat16)
    for k in range(1, planes):
        for e in range(local_experts):
            copies["h", k, e].start()

    for j in range(parts):
        cols = pl.ds(j * width, width)
        total = None
        for e in range(local_experts):
            for grads, weights in ((grads_g, wgv), (grads_u, wuv)):
                term = lax.dot_general(
                    grads[e], weights[e, cols, :], NT, preferred_element_type=jnp.float32
                )
                total = term if total is None else total + term
        total = total.reshape(chips, 2, rows, width)
        keep[j] = total[:, 0]
        pair_out[j] = total[:, 1].astype(jnp.bfloat16)
        copies["p", j].start()

    for k in range(1, planes):
        for d in range(1, chips):
            copies["d", k, d].wait_recv()
            copies["dc", k, d].start()

    for j in range(parts):
        copies["p", j].wait_recv()
        total = keep[j] + pair_in[j].astype(jnp.float32)
        keep[j, 0] = total[0]
        for d in range(1, chips):
            ret_out[j, d] = total[d].astype(jnp.bfloat16)
        for d in range(1, chips):
            copies["t", j, d].start()

    first = pl.multiple_of(plane * share, 16)
    for k in range(1, planes):
        for e in range(local_experts):
            copies["h", k, e].wait_recv()
        for d in range(chips):
            copies["dc", k, d].wait_recv()
    every = db[...].reshape(planes * count, model_width)
    for e in range(local_experts):
        pieces = [hid_out[e, pl.ds(first, share), :]] + [hid_in[k, e] for k in range(1, planes)]
        down_out[e] = jnp.dot(
            jnp.concatenate(pieces, axis=1), every, preferred_element_type=jnp.float32
        )

    for j in range(parts):
        total = keep[j, 0]
        for d in range(1, chips):
            copies["t", j, d].wait_recv()
            total = total + ret_in[j, d].astype(jnp.float32)
        token_out[:, pl.ds(j * width, width)] = total.astype(jnp.bfloat16)
    for c in copies.values():
        c.wait_send()


def fused_shapes(chips, planes, parts, rows, top, local_experts, model_width, hidden_units):
    bf16, f32 = jnp.bfloat16, jnp.float32
    count, width = 2 * chips * rows, model_width // parts
    return [
        ((2 * chips, rows, model_width), bf16),
        ((planes, 2 * chips, rows, model_width), bf16),
        ((2 * chips, rows, top), jnp.int32),
        ((2 * chips, rows, top), f32),
        ((local_experts, model_width, hidden_units), bf16),
        ((local_experts, model_width, hidden_units), bf16),
        ((local_experts, hidden_units, model_width), bf16),
        ((local_experts, count, hidden_units), f32),
        ((local_experts, count, hidden_units), f32),
        ((local_experts, hidden_units, count), bf16),
        ((planes, local_experts, hidden_units // planes, count), bf16),
        ((local_experts, count, hidden_units), bf16),
        ((local_experts, count, hidden_units), bf16),
        ((parts, chips, rows, width), f32),
        ((parts, chips, rows, width), bf16),
        ((parts, chips, rows, width), bf16),
        ((parts, chips, rows, width), bf16),
        ((parts, chips, rows, width), bf16),
    ]


def buffer_bytes(shapes):
    total = 0
    for dims, kind in shapes:
        size = jnp.dtype(kind).itemsize
        for dim in dims[:-1]:
            size *= dim
        total += size * (-(-dims[-1] // 128) * 128)
    return total


def plan(tokens, routes, w_gate):
    groups, planes = lax.axis_size("expert"), lax.axis_size("dp")
    chips, parts = groups // 2, 2
    rows, model_width = tokens.shape
    local_experts, _, hidden_units = w_gate.shape
    if groups % 2 or chips & (chips - 1) or planes & (planes - 1):
        return None
    if rows % 16 or hidden_units % (16 * planes) or (groups * rows) % 128 or model_width % (128 * parts):
        return None
    shapes = fused_shapes(
        chips, planes, parts, rows, routes.shape[1], local_experts, model_width, hidden_units
    )
    if buffer_bytes(shapes) > VMEM_BUDGET:
        return None
    return chips, planes, parts, shapes


def shards(tokens, out_grad, routes, route_gates, w_gate, w_up, w_down):
    planned = plan(tokens, routes, w_gate)
    if planned is None:
        return collective_shards(tokens, out_grad, routes, route_gates, w_gate, w_up, w_down)
    chips, planes, parts, shapes = planned
    rows, model_width = tokens.shape
    local_experts, _, hidden_units = w_gate.shape
    share = hidden_units // planes
    amount = len(copy_keys(chips, planes, local_experts, parts))
    vmem = pl.BlockSpec(memory_space=pltpu.VMEM)
    token_grad, down_grad = pl.pallas_call(
        functools.partial(fused_kernel, chips, planes, parts),
        out_shape=(
            jax.ShapeDtypeStruct((rows, model_width), jnp.bfloat16),
            jax.ShapeDtypeStruct((local_experts, share, model_width), jnp.float32),
        ),
        in_specs=[pl.BlockSpec(memory_space=pl.ANY)] * 7,
        out_specs=(vmem, vmem),
        scratch_shapes=[pltpu.VMEM(dims, kind) for dims, kind in shapes]
        + [
            pltpu.SemaphoreType.DMA((4 + 3 * local_experts,)),
            pltpu.SemaphoreType.DMA((amount,)),
            pltpu.SemaphoreType.DMA((amount,)),
        ],
        compiler_params=pltpu.CompilerParams(
            collective_id=0, has_side_effects=True, vmem_limit_bytes=60 << 20
        ),
        name="expert_backward",
    )(tokens, out_grad, routes, route_gates, w_gate, w_up, w_down)
    return (token_grad, down_grad.transpose(1, 0, 2))


def solution(mesh):
    placed = (
        P(("expert", "dp"), None),
        P(("expert", "dp"), None),
        P(("expert", "dp"), None),
        P(("expert", "dp"), None),
        P("expert", None, None),
        P("expert", None, None),
        P("expert", None, None),
    )
    return jax.shard_map(
        shards,
        mesh=mesh,
        in_specs=placed,
        out_specs=(P(("expert", "dp"), None), P("dp", "expert", None)),
        check_vma=False,
    )
```

```python
import functools

import jax
import jax.numpy as jnp
from jax import lax
from jax.experimental import pallas as pl
from jax.experimental.pallas import tpu as pltpu
from jax.sharding import PartitionSpec as P

VMEM_BUDGET = 44 << 20
STEPS = 4
NT = (((1,), (1,)), ((), ()))


def gate_up(arrived, w_gate, w_up):
    gate_pre = jnp.einsum("erd,edf->erf", arrived, w_gate, preferred_element_type=jnp.float32)
    up_pre = jnp.einsum("erd,edf->erf", arrived, w_up, preferred_element_type=jnp.float32)
    return (gate_pre, up_pre)


def collective_shards(tokens, out_grad, routes, route_gates, w_gate, w_up, w_down):
    tok_count, model_width = tokens.shape
    top_count = routes.shape[1]
    local_experts = w_gate.shape[0]
    groups = lax.axis_size("expert")
    experts = local_experts * groups
    slot_count = 2 * tok_count * top_count // experts
    flat_routes = routes.reshape(-1)
    onehot = (flat_routes[:, None] == jnp.arange(experts, dtype=jnp.int32)[None, :]).astype(
        jnp.int32
    )
    slot_rank = jnp.sum(onehot * (jnp.cumsum(onehot, axis=0) - onehot), axis=1)
    slot_index = flat_routes * slot_count + slot_rank
    placement = slot_index[None, :] == jnp.arange(experts * slot_count, dtype=jnp.int32)[:, None]
    route_place = placement.astype(jnp.bfloat16)
    token_place = jnp.sum(
        placement.reshape(experts * slot_count, tok_count, top_count).astype(jnp.float32), axis=2
    ).astype(jnp.bfloat16)
    send_inputs = (
        jnp.dot(token_place, tokens, preferred_element_type=jnp.float32)
        .astype(jnp.bfloat16)
        .reshape(experts, slot_count, model_width)
    )
    scaled = (
        (route_gates[:, :, None] * out_grad[:, None, :].astype(jnp.float32))
        .astype(jnp.bfloat16)
        .reshape(tok_count * top_count, model_width)
    )
    send_grads = (
        jnp.dot(route_place, scaled, preferred_element_type=jnp.float32)
        .astype(jnp.bfloat16)
        .reshape(experts, slot_count, model_width)
    )
    arrived, arrived_grad = (
        lax.all_to_all(send_inputs, "expert", split_axis=0, concat_axis=1, tiled=True),
        lax.all_to_all(send_grads, "expert", split_axis=0, concat_axis=1, tiled=True),
    )
    gate_pre, up_pre = gate_up(arrived, w_gate, w_up)
    sigmoid_gate = jax.nn.sigmoid(gate_pre)
    silu_gate = gate_pre * sigmoid_gate
    hidden = (silu_gate * up_pre).astype(jnp.bfloat16)
    hidden_grad = jnp.einsum(
        "erd,efd->erf", arrived_grad, w_down, preferred_element_type=jnp.float32
    )
    gate_grad = (
        hidden_grad * up_pre * (sigmoid_gate + gate_pre * sigmoid_gate * (1.0 - sigmoid_gate))
    ).astype(jnp.bfloat16)
    up_grad = (hidden_grad * silu_gate).astype(jnp.bfloat16)
    row_grads = (
        jnp.einsum("erf,edf->erd", gate_grad, w_gate, preferred_element_type=jnp.float32)
        + jnp.einsum("erf,edf->erd", up_grad, w_up, preferred_element_type=jnp.float32)
    ).astype(jnp.bfloat16)
    returned = lax.all_to_all(row_grads, "expert", split_axis=1, concat_axis=0, tiled=True)
    token_grad = lax.dot_general(
        token_place,
        returned.reshape(experts * slot_count, model_width),
        (((0,), (0,)), ((), ())),
        preferred_element_type=jnp.float32,
    ).astype(jnp.bfloat16)
    hidden_units = hidden.shape[2]
    share_rows = hidden_units // lax.axis_size("dp")
    partial_grad = jnp.einsum(
        "erf,erd->fed", hidden, arrived_grad, preferred_element_type=jnp.float32
    ).astype(jnp.bfloat16)
    total_grad = lax.psum(partial_grad, "dp").astype(jnp.float32)
    first_row = lax.axis_index("dp") * share_rows
    down_grad = lax.dynamic_slice_in_dim(total_grad, first_row, share_rows, 0)
    return (token_grad, down_grad)


def flip(index, bits):
    out, step = index, 1
    while step <= bits:
        if bits & step:
            out = out + step * (1 - 2 * ((index // step) % 2))
        step *= 2
    return out


def copy_keys(chips, planes, local_experts, parts):
    keys = []
    for name in ("x", "r", "g"):
        keys += [(name, d) for d in range(1, chips)] + [(name + "c", d) for d in range(chips)]
    keys += [("z", k) for k in range(1, planes)]
    keys += [("d", k, d) for k in range(planes) for d in range(1, chips)]
    keys += [("dc", k, d) for k in range(planes) for d in range(chips)]
    keys += [("h", k, e) for k in range(1, planes) for e in range(local_experts)]
    keys += [("p", j) for j in range(parts)]
    keys += [("t", j, d) for j in range(parts) for d in range(1, chips)]
    return {key: i for i, key in enumerate(keys)}


def fused_kernel(
    chips, planes, parts, tok, dy, rt, gt, wg, wu, wd, every, hid_in, own_sum, ret_in,
    xb, db, rb, gb, wgv, wuv, wdv, gates, ups, hid_out, grads_g, grads_u,
    keep, pair_out, pair_in, ret_out, lsem, ssem, rsem,
):
    local_experts, model_width, hidden_units = wg.shape
    rows = tok.shape[0]
    count = 2 * chips * rows
    share = hidden_units // planes
    width = model_width // parts
    me, plane = lax.axis_index("expert"), lax.axis_index("dp")
    chip, core = me // 2, me % 2
    partner = {"expert": chip * 2 + 1 - core, "dp": plane}
    across = [{"expert": flip(chip, d) * 2 + core, "dp": plane} for d in range(chips)]
    above = [{"expert": me, "dp": flip(plane, k)} for k in range(planes)]
    keys = copy_keys(chips, planes, local_experts, parts)

    local = []

    def load(src, dst):
        c = pltpu.make_async_copy(src, dst, lsem.at[len(local)])
        c.start()
        local.append(c)
        return c

    own = [load(tok, xb.at[0]), load(rt, rb.at[0]), load(gt, gb.at[0]), load(dy, db.at[0])]
    gate_up_loads = [(load(wg.at[e], wgv.at[e]), load(wu.at[e], wuv.at[e])) for e in range(local_experts)]
    down_loads = [load(wd.at[e], wdv.at[e]) for e in range(local_experts)]

    def remote(key, src, dst, target):
        i = keys[key]
        return pltpu.make_async_remote_copy(
            src_ref=src, dst_ref=dst, send_sem=ssem.at[i], recv_sem=rsem.at[i],
            device_id=target, device_id_type=pl.DeviceIdType.MESH,
        )

    copies = {}
    for name, src, buf in (("x", tok, xb), ("r", rt, rb), ("g", gt, gb)):
        for d in range(chips):
            if d:
                copies[name, d] = remote((name, d), src, buf.at[2 * d], across[d])
            copies[name + "c", d] = remote(
                (name + "c", d), buf.at[2 * d] if d else src, buf.at[2 * d + 1], partner
            )
    for k in range(planes):
        blocks = every.at[k] if k else db
        if k:
            copies["z", k] = remote(("z", k), dy, blocks.at[0], above[k])
        first = blocks.at[0] if k else dy
        for d in range(chips):
            if k and d == chips - 1:
                copies["d", k, d] = remote(("d", k, d), db.at[2 * d], blocks.at[2 * d], above[k])
            elif d:
                copies["d", k, d] = remote(("d", k, d), first, blocks.at[2 * d], across[d])
            copies["dc", k, d] = remote(
                ("dc", k, d), blocks.at[2 * d] if d else first, blocks.at[2 * d + 1], partner
            )
    for k in range(1, planes):
        first = pl.multiple_of(flip(plane, k) * share, 16)
        for e in range(local_experts):
            copies["h", k, e] = remote(
                ("h", k, e), hid_out.at[e, pl.ds(first, share)], hid_in.at[k, e], above[k]
            )
    for j in range(parts):
        copies["p", j] = remote(("p", j), pair_out.at[j], pair_in.at[j], partner)
        for d in range(1, chips):
            copies["t", j, d] = remote(
                ("t", j, d), ret_out.at[j, d], ret_in.at[d - 1, :, pl.ds(j * width, width)], across[d]
            )

    barrier = pltpu.get_barrier_semaphore()
    targets = [partner] + across[1:] + above[1:]
    for target in targets:
        pl.semaphore_signal(barrier, inc=1, device_id=target, device_id_type=pl.DeviceIdType.MESH)
    pl.semaphore_wait(barrier, len(targets))

    for name in ("x", "r", "g"):
        for d in range(1, chips):
            copies[name, d].start()
    for k in range(planes - 1, 0, -1):
        copies["z", k].start()
    for d in range(1, chips):
        copies["d", 0, d].start()
    for name in ("x", "r", "g"):
        copies[name + "c", 0].start()
    copies["dc", 0, 0].start()

    for d in range(1, chips):
        for name in ("x", "r", "g"):
            copies[name, d].wait_recv()
            copies[name + "c", d].start()
    for c in own:
        c.wait()
    for d in range(chips):
        for name in ("x", "r", "g"):
            copies[name + "c", d].wait_recv()

    x = xb[...].reshape(count, model_width)
    for e in range(local_experts):
        for c in gate_up_loads[e]:
            c.wait()
        gates[e] = jnp.dot(x, wgv[e], preferred_element_type=jnp.float32)
        ups[e] = jnp.dot(x, wuv[e], preferred_element_type=jnp.float32)
        if e == 0:
            for d in range(1, chips):
                copies["d", 0, d].wait_recv()
                copies["dc", 0, d].start()
            for k in range(1, planes):
                copies["d", k, chips - 1].start()
            for k in range(1, planes):
                copies["z", k].wait_recv()
                for d in range(1, chips - 1):
                    copies["d", k, d].start()
                copies["dc", k, 0].start()
    for d in range(chips):
        copies["dc", 0, d].wait_recv()
    load(db, every.at[0])

    named, given = rb[...], gb[...]
    diagonal = lax.broadcasted_iota(jnp.int32, (1, rows, rows), 1) == lax.broadcasted_iota(
        jnp.int32, (1, rows, rows), 2
    )
    grad_rows = db[...].reshape(count, model_width)
    for e in range(local_experts):
        down_loads[e].wait()
        gain = jnp.sum(
            jnp.where(named == me * local_experts + e, given, 0.0), axis=1, keepdims=True
        )
        gain = jnp.sum(jnp.where(diagonal, gain, 0.0), axis=2, keepdims=True).reshape(count, 1)
        hidden_grad = gain * lax.dot_general(
            grad_rows, wdv[e], NT, preferred_element_type=jnp.float32
        )
        gate_pre, up_pre = gates[e], ups[e]
        s = jax.nn.sigmoid(gate_pre)
        silu = gate_pre * s
        hid_out[e] = (silu * up_pre * gain).T.astype(jnp.bfloat16)
        grads_g[e] = (hidden_grad * up_pre * (s + gate_pre * s * (1.0 - s))).astype(jnp.bfloat16)
        grads_u[e] = (hidden_grad * silu).astype(jnp.bfloat16)
    for k in range(1, planes):
        for e in range(local_experts):
            copies["h", k, e].start()
    first = pl.multiple_of(plane * share, 16)
    for e in range(local_experts):
        load(hid_out.at[e, pl.ds(first, share)], hid_in.at[0, e])

    for j in range(parts):
        cols = pl.ds(j * width, width)
        total = None
        for e in range(local_experts):
            for grads, weights in ((grads_g, wgv), (grads_u, wuv)):
                term = lax.dot_general(
                    grads[e], weights[e, cols, :], NT, preferred_element_type=jnp.float32
                )
                total = term if total is None else total + term
        total = total.reshape(chips, 2, rows, width)
        keep[j] = total[:, 0]
        pair_out[j] = total[:, 1].astype(jnp.bfloat16)
        copies["p", j].start()

    for k in range(1, planes):
        for d in range(1, chips):
            copies["d", k, d].wait_recv()
            copies["dc", k, d].start()

    for j in range(parts):
        copies["p", j].wait_recv()
        total = keep[j] + pair_in[j].astype(jnp.float32)
        keep[j, 0] = total[0]
        load(keep.at[j, 0], own_sum.at[:, pl.ds(j * width, width)])
        for d in range(1, chips):
            ret_out[j, d] = total[d].astype(jnp.bfloat16)
        for d in range(1, chips):
            copies["t", j, d].start()

    for k in range(1, planes):
        for e in range(local_experts):
            copies["h", k, e].wait_recv()
        for d in range(chips):
            copies["dc", k, d].wait_recv()
    for j in range(parts):
        for d in range(1, chips):
            copies["t", j, d].wait_recv()
    for c in local[len(own) + 3 * local_experts :]:
        c.wait()
    for c in copies.values():
        c.wait_send()


def finish_kernel(every, hid, own_sum, returned, token_out, down_out):
    planes, local_experts, share, _ = hid.shape
    blocks = every.shape[1] // 128
    lines = down_out.reshape(share * blocks * local_experts, 128)
    for e in range(local_experts):
        pieces = jnp.concatenate([hid[k, e] for k in range(planes)], axis=1)
        result = jnp.dot(pieces, every[...], preferred_element_type=jnp.float32)
        for b in range(blocks):
            lines[pl.ds(b * local_experts + e, share, stride=blocks * local_experts), :] = (
                result[:, b * 128 : (b + 1) * 128]
            )
    total = own_sum[...]
    for d in range(returned.shape[0]):
        total = total + returned[d].astype(jnp.float32)
    token_out[...] = total.astype(jnp.bfloat16)


def fused_shapes(chips, planes, parts, rows, top, local_experts, model_width, hidden_units):
    bf16, f32 = jnp.bfloat16, jnp.float32
    count, width = 2 * chips * rows, model_width // parts
    return [
        ((2 * chips, rows, model_width), bf16),
        ((2 * chips, rows, model_width), bf16),
        ((2 * chips, top, rows), jnp.int32),
        ((2 * chips, top, rows), f32),
        ((local_experts, model_width, hidden_units), bf16),
        ((local_experts, model_width, hidden_units), bf16),
        ((local_experts, hidden_units, model_width), bf16),
        ((local_experts, count, hidden_units), f32),
        ((local_experts, count, hidden_units), f32),
        ((local_experts, hidden_units, count), bf16),
        ((local_experts, count, hidden_units), bf16),
        ((local_experts, count, hidden_units), bf16),
        ((parts, chips, rows, width), f32),
        ((parts, chips, rows, width), bf16),
        ((parts, chips, rows, width), bf16),
        ((parts, chips, rows, width), bf16),
    ]


def buffer_bytes(shapes):
    total = 0
    for dims, kind in shapes:
        size = jnp.dtype(kind).itemsize
        for dim in dims[:-1]:
            size *= dim
        total += size * (-(-dims[-1] // 128) * 128)
    return total


def plan(tokens, routes, w_gate):
    groups, planes = lax.axis_size("expert"), lax.axis_size("dp")
    chips, parts = groups // 2, 2
    rows, model_width = tokens.shape
    local_experts, _, hidden_units = w_gate.shape
    if groups % 2 or chips & (chips - 1) or planes & (planes - 1):
        return None
    if rows % 16 or hidden_units % (16 * planes) or (groups * rows) % 128 or model_width % (512 * STEPS):
        return None
    shapes = fused_shapes(
        chips, planes, parts, rows, routes.shape[1], local_experts, model_width, hidden_units
    )
    if buffer_bytes(shapes) > VMEM_BUDGET:
        return None
    return chips, planes, parts, shapes


def shards(tokens, out_grad, routes, route_gates, w_gate, w_up, w_down):
    planned = plan(tokens, routes, w_gate)
    if planned is None:
        return collective_shards(tokens, out_grad, routes, route_gates, w_gate, w_up, w_down)
    chips, planes, parts, shapes = planned
    rows, model_width = tokens.shape
    local_experts, _, hidden_units = w_gate.shape
    share = hidden_units // planes
    amount = len(copy_keys(chips, planes, local_experts, parts))
    count = 2 * chips * rows
    anywhere = pl.BlockSpec(memory_space=pl.ANY)
    every, hid, own_sum, returned = pl.pallas_call(
        functools.partial(fused_kernel, chips, planes, parts),
        out_shape=(
            jax.ShapeDtypeStruct((planes, 2 * chips, rows, model_width), jnp.bfloat16),
            jax.ShapeDtypeStruct((planes, local_experts, share, count), jnp.bfloat16),
            jax.ShapeDtypeStruct((rows, model_width), jnp.float32),
            jax.ShapeDtypeStruct((chips - 1, rows, model_width), jnp.bfloat16),
        ),
        in_specs=[anywhere] * 7,
        out_specs=(anywhere,) * 4,
        scratch_shapes=[pltpu.VMEM(dims, kind) for dims, kind in shapes]
        + [
            pltpu.SemaphoreType.DMA((5 + 4 * local_experts + parts,)),
            pltpu.SemaphoreType.DMA((amount,)),
            pltpu.SemaphoreType.DMA((amount,)),
        ],
        compiler_params=pltpu.CompilerParams(
            collective_id=0, has_side_effects=True, vmem_limit_bytes=60 << 20
        ),
        name="expert_backward",
    )(tokens, out_grad, routes.T, route_gates.T, w_gate, w_up, w_down)
    width = model_width // STEPS
    lines = width // 128 * local_experts
    token_grad, down_grad = pl.pallas_call(
        finish_kernel,
        grid=(STEPS,),
        out_shape=(
            jax.ShapeDtypeStruct((rows, model_width), jnp.bfloat16),
            jax.ShapeDtypeStruct((share, model_width // 128 * local_experts, 128), jnp.float32),
        ),
        in_specs=[
            pl.BlockSpec((planes * count, width), lambda i: (0, i)),
            pl.BlockSpec((planes, local_experts, share, count), lambda i: (0, 0, 0, 0)),
            pl.BlockSpec((rows, width), lambda i: (0, i)),
            pl.BlockSpec((chips - 1, rows, width), lambda i: (0, 0, i)),
        ],
        out_specs=(
            pl.BlockSpec((rows, width), lambda i: (0, i)),
            pl.BlockSpec((share, lines, 128), lambda i: (0, i, 0)),
        ),
        name="expert_finish",
    )(every.reshape(planes * count, model_width), hid, own_sum, returned)
    down_grad = down_grad.reshape(share, model_width // 128, local_experts, 128)
    return (token_grad, down_grad.transpose(0, 2, 1, 3).reshape(share, local_experts, model_width))


def solution(mesh):
    placed = (
        P(("expert", "dp"), None),
        P(("expert", "dp"), None),
        P(("expert", "dp"), None),
        P(("expert", "dp"), None),
        P("expert", None, None),
        P("expert", None, None),
        P("expert", None, None),
    )
    return jax.shard_map(
        shards,
        mesh=mesh,
        in_specs=placed,
        out_specs=(P(("expert", "dp"), None), P("dp", "expert", None)),
        check_vma=False,
    )
```

```python
import functools

import jax
import jax.numpy as jnp
from jax import lax
from jax.experimental import pallas as pl
from jax.experimental.pallas import tpu as pltpu
from jax.sharding import PartitionSpec as P

VMEM_BUDGET = 44 << 20
STEPS = 2
ALONG = 1
LAG = 1
NAMES = ("r", "g", "x0", "x1")
NT = (((1,), (1,)), ((), ()))


def gate_up(arrived, w_gate, w_up):
    gate_pre = jnp.einsum("erd,edf->erf", arrived, w_gate, preferred_element_type=jnp.float32)
    up_pre = jnp.einsum("erd,edf->erf", arrived, w_up, preferred_element_type=jnp.float32)
    return (gate_pre, up_pre)


def collective_shards(tokens, out_grad, routes, route_gates, w_gate, w_up, w_down):
    tok_count, model_width = tokens.shape
    top_count = routes.shape[1]
    local_experts = w_gate.shape[0]
    groups = lax.axis_size("expert")
    experts = local_experts * groups
    slot_count = 2 * tok_count * top_count // experts
    flat_routes = routes.reshape(-1)
    onehot = (flat_routes[:, None] == jnp.arange(experts, dtype=jnp.int32)[None, :]).astype(
        jnp.int32
    )
    slot_rank = jnp.sum(onehot * (jnp.cumsum(onehot, axis=0) - onehot), axis=1)
    slot_index = flat_routes * slot_count + slot_rank
    placement = slot_index[None, :] == jnp.arange(experts * slot_count, dtype=jnp.int32)[:, None]
    route_place = placement.astype(jnp.bfloat16)
    token_place = jnp.sum(
        placement.reshape(experts * slot_count, tok_count, top_count).astype(jnp.float32), axis=2
    ).astype(jnp.bfloat16)
    send_inputs = (
        jnp.dot(token_place, tokens, preferred_element_type=jnp.float32)
        .astype(jnp.bfloat16)
        .reshape(experts, slot_count, model_width)
    )
    scaled = (
        (route_gates[:, :, None] * out_grad[:, None, :].astype(jnp.float32))
        .astype(jnp.bfloat16)
        .reshape(tok_count * top_count, model_width)
    )
    send_grads = (
        jnp.dot(route_place, scaled, preferred_element_type=jnp.float32)
        .astype(jnp.bfloat16)
        .reshape(experts, slot_count, model_width)
    )
    arrived, arrived_grad = (
        lax.all_to_all(send_inputs, "expert", split_axis=0, concat_axis=1, tiled=True),
        lax.all_to_all(send_grads, "expert", split_axis=0, concat_axis=1, tiled=True),
    )
    gate_pre, up_pre = gate_up(arrived, w_gate, w_up)
    sigmoid_gate = jax.nn.sigmoid(gate_pre)
    silu_gate = gate_pre * sigmoid_gate
    hidden = (silu_gate * up_pre).astype(jnp.bfloat16)
    hidden_grad = jnp.einsum(
        "erd,efd->erf", arrived_grad, w_down, preferred_element_type=jnp.float32
    )
    gate_grad = (
        hidden_grad * up_pre * (sigmoid_gate + gate_pre * sigmoid_gate * (1.0 - sigmoid_gate))
    ).astype(jnp.bfloat16)
    up_grad = (hidden_grad * silu_gate).astype(jnp.bfloat16)
    row_grads = (
        jnp.einsum("erf,edf->erd", gate_grad, w_gate, preferred_element_type=jnp.float32)
        + jnp.einsum("erf,edf->erd", up_grad, w_up, preferred_element_type=jnp.float32)
    ).astype(jnp.bfloat16)
    returned = lax.all_to_all(row_grads, "expert", split_axis=1, concat_axis=0, tiled=True)
    token_grad = lax.dot_general(
        token_place,
        returned.reshape(experts * slot_count, model_width),
        (((0,), (0,)), ((), ())),
        preferred_element_type=jnp.float32,
    ).astype(jnp.bfloat16)
    hidden_units = hidden.shape[2]
    share_rows = hidden_units // lax.axis_size("dp")
    partial_grad = jnp.einsum(
        "erf,erd->fed", hidden, arrived_grad, preferred_element_type=jnp.float32
    ).astype(jnp.bfloat16)
    total_grad = lax.psum(partial_grad, "dp").astype(jnp.float32)
    first_row = lax.axis_index("dp") * share_rows
    down_grad = lax.dynamic_slice_in_dim(total_grad, first_row, share_rows, 0)
    return (token_grad, down_grad)


def flip(index, bits):
    out, step = index, 1
    while step <= bits:
        if bits & step:
            out = out + step * (1 - 2 * ((index // step) % 2))
        step *= 2
    return out


def copy_keys(chips, planes, local_experts, parts):
    keys = []
    for name in NAMES:
        keys += [(name, d) for d in range(1, chips)] + [(name + "c", d) for d in range(chips)]
    keys += [("z", k) for k in range(1, planes)]
    keys += [("d", k, d) for k in range(planes) for d in range(1, chips)]
    keys += [("dc", k, d) for k in range(planes) for d in range(chips)]
    keys += [("h", k, e) for k in range(1, planes) for e in range(local_experts)]
    keys += [("p", j) for j in range(parts)]
    keys += [("t", j, d) for j in range(parts) for d in range(1, chips)]
    return {key: i for i, key in enumerate(keys)}


def fused_kernel(
    chips, planes, parts, tok, dy, rt, gt, wg, wu, wd, every, hid_in, own_sum, ret_in,
    xb, db, rb, gb, wgv, wuv, wdv, gates, ups, grads, hid_out, grads_g, grads_u,
    keep, pair_out, pair_in, ret_out, lsem, ssem, rsem,
):
    local_experts, model_width, hidden_units = wg.shape
    rows = tok.shape[0]
    count = 2 * chips * rows
    share = hidden_units // planes
    width = model_width // parts
    me, plane = lax.axis_index("expert"), lax.axis_index("dp")
    chip, core = me // 2, me % 2
    partner = {"expert": chip * 2 + 1 - core, "dp": plane}
    across = [{"expert": flip(chip, d) * 2 + core, "dp": plane} for d in range(chips)]
    above = [{"expert": me, "dp": flip(plane, k)} for k in range(planes)]
    keys = copy_keys(chips, planes, local_experts, parts)

    local = []

    def load(src, dst):
        c = pltpu.make_async_copy(src, dst, lsem.at[len(local)])
        c.start()
        local.append(c)
        return c

    own = [load(tok, xb.at[0]), load(rt, rb.at[0]), load(gt, gb.at[0]), load(dy, db.at[0])]
    gate_up_loads = [(load(wg.at[e], wgv.at[e]), load(wu.at[e], wuv.at[e])) for e in range(local_experts)]
    down_loads = [load(wd.at[e], wdv.at[e]) for e in range(local_experts)]

    def remote(key, src, dst, target):
        i = keys[key]
        return pltpu.make_async_remote_copy(
            src_ref=src, dst_ref=dst, send_sem=ssem.at[i], recv_sem=rsem.at[i],
            device_id=target, device_id_type=pl.DeviceIdType.MESH,
        )

    copies = {}
    half = model_width // 2
    for name in NAMES:
        src, buf = {"r": (rt, rb), "g": (gt, gb)}.get(name, (tok, xb))
        cols = pl.ds(int(name[1]) * half, half) if name[0] == "x" else slice(None)
        src = src.at[:, cols]
        for d in range(chips):
            if d:
                copies[name, d] = remote((name, d), src, buf.at[2 * d, :, cols], across[d])
            copies[name + "c", d] = remote(
                (name + "c", d), buf.at[2 * d, :, cols] if d else src, buf.at[2 * d + 1, :, cols], partner
            )
    for k in range(planes):
        blocks = every.at[k] if k else db
        if k:
            copies["z", k] = remote(("z", k), dy, blocks.at[0], above[k])
        first = blocks.at[0] if k else dy
        for d in range(chips):
            if 0 < k <= ALONG and d == chips - 1:
                copies["d", k, d] = remote(("d", k, d), db.at[2 * d], blocks.at[2 * d], above[k])
            elif d:
                copies["d", k, d] = remote(("d", k, d), first, blocks.at[2 * d], across[d])
            copies["dc", k, d] = remote(
                ("dc", k, d), blocks.at[2 * d] if d else first, blocks.at[2 * d + 1], partner
            )
    for k in range(1, planes):
        first = pl.multiple_of(flip(plane, k) * share, 16)
        for e in range(local_experts):
            copies["h", k, e] = remote(
                ("h", k, e), hid_out.at[e, pl.ds(first, share)], hid_in.at[k, e], above[k]
            )
    for j in range(parts):
        copies["p", j] = remote(("p", j), pair_out.at[j], pair_in.at[j], partner)
        for d in range(1, chips):
            copies["t", j, d] = remote(
                ("t", j, d), ret_out.at[j, d], ret_in.at[d - 1, :, pl.ds(j * width, width)], across[d]
            )

    barrier = pltpu.get_barrier_semaphore()
    targets = [partner] + across[1:] + above[1:]
    for target in targets:
        pl.semaphore_signal(barrier, inc=1, device_id=target, device_id_type=pl.DeviceIdType.MESH)
    pl.semaphore_wait(barrier, len(targets))

    for d in range(chips - 1, 0, -1):
        copies["d", 0, d].start()
    for k in range(planes - 1, 0, -1):
        copies["z", k].start()
    for name in NAMES:
        for d in range(chips - 1, 0, -1):
            copies[name, d].start()
    copies["dc", 0, 0].start()
    for name in NAMES:
        copies[name + "c", 0].start()
    for d in range(chips - 1, 0, -1):
        copies["d", 0, d].wait_recv()
        copies["dc", 0, d].start()
        if d == chips - 1:
            for k in range(1, min(planes, ALONG + 1)):
                copies["d", k, d].start()
    for k in range(1, planes):
        copies["z", k].wait_recv()
        for d in range(chips - 1, 0, -1):
            if d < chips - 1 or k > ALONG:
                copies["d", k, d].start()
        copies["dc", k, 0].start()
    for c in own:
        c.wait()
    for d in range(chips):
        copies["dc", 0, d].wait_recv()
    load(db, every.at[0])
    grad_rows = db[...].reshape(count, model_width)
    for e in range(local_experts):
        down_loads[e].wait()
        grads[e] = lax.dot_general(grad_rows, wdv[e], NT, preferred_element_type=jnp.float32)

    for name in NAMES:
        for d in range(chips - 1, 0, -1):
            copies[name, d].wait_recv()
            copies[name + "c", d].start()
    for name in NAMES:
        for d in range(chips):
            copies[name + "c", d].wait_recv()
        if name[0] == "x":
            begin = int(name[1]) * half
            x = xb[:, :, begin : begin + half].reshape(count, half)
            for e in range(local_experts):
                if begin == 0:
                    for c in gate_up_loads[e]:
                        c.wait()
                for pre, weights in ((gates, wgv), (ups, wuv)):
                    term = jnp.dot(
                        x, weights[e, begin : begin + half, :], preferred_element_type=jnp.float32
                    )
                    pre[e] = term if begin == 0 else pre[e] + term

    named, given = rb[...], gb[...]
    diagonal = lax.broadcasted_iota(jnp.int32, (1, rows, rows), 1) == lax.broadcasted_iota(
        jnp.int32, (1, rows, rows), 2
    )
    for e in range(local_experts):
        gain = jnp.sum(
            jnp.where(named == me * local_experts + e, given, 0.0), axis=1, keepdims=True
        )
        gain = jnp.sum(jnp.where(diagonal, gain, 0.0), axis=2, keepdims=True).reshape(count, 1)
        hidden_grad = gain * grads[e]
        gate_pre, up_pre = gates[e], ups[e]
        s = jax.nn.sigmoid(gate_pre)
        silu = gate_pre * s
        ups[e] = silu * up_pre * gain
        grads_g[e] = (hidden_grad * up_pre * (s + gate_pre * s * (1.0 - s))).astype(jnp.bfloat16)
        grads_u[e] = (hidden_grad * silu).astype(jnp.bfloat16)

    for j in range(parts + LAG):
        if j < parts:
            cols = pl.ds(j * width, width)
            total = None
            for e in range(local_experts):
                for rows_grad, weights in ((grads_g, wgv), (grads_u, wuv)):
                    term = lax.dot_general(
                        rows_grad[e], weights[e, cols, :], NT, preferred_element_type=jnp.float32
                    )
                    total = term if total is None else total + term
            total = total.reshape(chips, 2, rows, width)
            pair_out[j] = total[:, 1].astype(jnp.bfloat16)
            copies["p", j].start()
            keep[j] = total[:, 0]
        if j == parts - 1:
            for e in range(local_experts):
                hid_out[e] = ups[e].T.astype(jnp.bfloat16)
            for k in range(1, planes):
                for e in range(local_experts):
                    copies["h", k, e].start()
            first = pl.multiple_of(plane * share, 16)
            for e in range(local_experts):
                load(hid_out.at[e, pl.ds(first, share)], hid_in.at[0, e])
        if j >= LAG:
            i = j - LAG
            copies["p", i].wait_recv()
            total = keep[i] + pair_in[i].astype(jnp.float32)
            for d in range(chips - 1, 0, -1):
                ret_out[i, d] = total[d].astype(jnp.bfloat16)
            for d in range(chips - 1, 0, -1):
                copies["t", i, d].start()
            keep[i, 0] = total[0]
            load(keep.at[i, 0], own_sum.at[:, pl.ds(i * width, width)])

    for k in range(1, planes):
        for d in range(1, chips):
            copies["d", k, d].wait_recv()
            copies["dc", k, d].start()

    for k in range(1, planes):
        for e in range(local_experts):
            copies["h", k, e].wait_recv()
        for d in range(chips):
            copies["dc", k, d].wait_recv()
    for j in range(parts):
        for d in range(1, chips):
            copies["t", j, d].wait_recv()
    for c in local[len(own) + 3 * local_experts :]:
        c.wait()
    for c in copies.values():
        c.wait_send()


def finish_kernel(
    every, hid, own_sum, returned, token_out, down_out,
    every_v, hid_v, own_v, returned_v, token_v, down_v, sems,
):
    planes, local_experts, share, count = hid.shape
    width = every.shape[1] // STEPS
    blocks = width // 128
    started = []

    def copy(src, dst):
        c = pltpu.make_async_copy(src, dst, sems.at[len(started)])
        c.start()
        started.append(c)
        return c

    hid_load = copy(hid, hid_v)
    loads = [
        copy(every.at[:, pl.ds(i * width, width)], every_v.at[:, pl.ds(i * width, width)])
        for i in range(STEPS)
    ]
    last_loads = [copy(own_sum, own_v), copy(returned, returned_v)]
    hid_load.wait()
    pieces = [hid_v[k].reshape(local_experts * share, count) for k in range(planes)]
    pieces = jnp.concatenate(pieces, axis=1)
    stores = []
    for i in range(STEPS):
        loads[i].wait()
        result = jnp.dot(
            pieces, every_v[:, i * width : (i + 1) * width], preferred_element_type=jnp.float32
        )
        lines = down_v.at[i].reshape(share * blocks * local_experts, 128)
        for e in range(local_experts):
            for b in range(blocks):
                lines[pl.ds(b * local_experts + e, share, stride=blocks * local_experts), :] = (
                    result[e * share : (e + 1) * share, b * 128 : (b + 1) * 128]
                )
        stores.append(
            copy(down_v.at[i], down_out.at[:, pl.ds(i * blocks * local_experts, blocks * local_experts)])
        )
        if i == 0:
            for c in last_loads:
                c.wait()
            total = own_v[...]
            for d in range(returned.shape[0]):
                total = total + returned_v[d].astype(jnp.float32)
            token_v[...] = total.astype(jnp.bfloat16)
            stores.append(copy(token_v, token_out))
    for c in stores:
        c.wait()


def fused_shapes(chips, planes, parts, rows, top, local_experts, model_width, hidden_units):
    bf16, f32 = jnp.bfloat16, jnp.float32
    count, width = 2 * chips * rows, model_width // parts
    return [
        ((2 * chips, rows, model_width), bf16),
        ((2 * chips, rows, model_width), bf16),
        ((2 * chips, top, rows), jnp.int32),
        ((2 * chips, top, rows), f32),
        ((local_experts, model_width, hidden_units), bf16),
        ((local_experts, model_width, hidden_units), bf16),
        ((local_experts, hidden_units, model_width), bf16),
        ((local_experts, count, hidden_units), f32),
        ((local_experts, count, hidden_units), f32),
        ((local_experts, count, hidden_units), f32),
        ((local_experts, hidden_units, count), bf16),
        ((local_experts, count, hidden_units), bf16),
        ((local_experts, count, hidden_units), bf16),
        ((parts, chips, rows, width), f32),
        ((parts, chips, rows, width), bf16),
        ((parts, chips, rows, width), bf16),
        ((parts, chips, rows, width), bf16),
    ]


def buffer_bytes(shapes):
    total = 0
    for dims, kind in shapes:
        size = jnp.dtype(kind).itemsize
        for dim in dims[:-1]:
            size *= dim
        total += size * (-(-dims[-1] // 128) * 128)
    return total


def plan(tokens, routes, w_gate):
    groups, planes = lax.axis_size("expert"), lax.axis_size("dp")
    chips, parts = groups // 2, 2
    rows, model_width = tokens.shape
    local_experts, _, hidden_units = w_gate.shape
    if groups % 2 or chips & (chips - 1) or planes & (planes - 1):
        return None
    if rows % 16 or hidden_units % (16 * planes) or (groups * rows) % 128 or model_width % (512 * STEPS):
        return None
    shapes = fused_shapes(
        chips, planes, parts, rows, routes.shape[1], local_experts, model_width, hidden_units
    )
    if buffer_bytes(shapes) > VMEM_BUDGET:
        return None
    return chips, planes, parts, shapes


def shards(tokens, out_grad, routes, route_gates, w_gate, w_up, w_down):
    planned = plan(tokens, routes, w_gate)
    if planned is None:
        return collective_shards(tokens, out_grad, routes, route_gates, w_gate, w_up, w_down)
    chips, planes, parts, shapes = planned
    rows, model_width = tokens.shape
    local_experts, _, hidden_units = w_gate.shape
    share = hidden_units // planes
    amount = len(copy_keys(chips, planes, local_experts, parts))
    count = 2 * chips * rows
    anywhere = pl.BlockSpec(memory_space=pl.ANY)
    every, hid, own_sum, returned = pl.pallas_call(
        functools.partial(fused_kernel, chips, planes, parts),
        out_shape=(
            jax.ShapeDtypeStruct((planes, 2 * chips, rows, model_width), jnp.bfloat16),
            jax.ShapeDtypeStruct((planes, local_experts, share, count), jnp.bfloat16),
            jax.ShapeDtypeStruct((rows, model_width), jnp.float32),
            jax.ShapeDtypeStruct((chips - 1, rows, model_width), jnp.bfloat16),
        ),
        in_specs=[anywhere] * 7,
        out_specs=(anywhere,) * 4,
        scratch_shapes=[pltpu.VMEM(dims, kind) for dims, kind in shapes]
        + [
            pltpu.SemaphoreType.DMA((5 + 4 * local_experts + parts,)),
            pltpu.SemaphoreType.DMA((amount,)),
            pltpu.SemaphoreType.DMA((amount,)),
        ],
        compiler_params=pltpu.CompilerParams(
            collective_id=0, has_side_effects=True, vmem_limit_bytes=60 << 20
        ),
        name="expert_backward",
    )(tokens, out_grad, routes.T, route_gates.T, w_gate, w_up, w_down)
    width = model_width // STEPS
    lines = width // 128 * local_experts
    token_grad, down_grad = pl.pallas_call(
        finish_kernel,
        out_shape=(
            jax.ShapeDtypeStruct((rows, model_width), jnp.bfloat16),
            jax.ShapeDtypeStruct((share, model_width // 128 * local_experts, 128), jnp.float32),
        ),
        in_specs=[anywhere] * 4,
        out_specs=(anywhere,) * 2,
        scratch_shapes=[
            pltpu.VMEM((planes * count, model_width), jnp.bfloat16),
            pltpu.VMEM(hid.shape, jnp.bfloat16),
            pltpu.VMEM((rows, model_width), jnp.float32),
            pltpu.VMEM((chips - 1, rows, model_width), jnp.bfloat16),
            pltpu.VMEM((rows, model_width), jnp.bfloat16),
            pltpu.VMEM((STEPS, share, lines, 128), jnp.float32),
            pltpu.SemaphoreType.DMA((4 + 2 * STEPS,)),
        ],
        compiler_params=pltpu.CompilerParams(vmem_limit_bytes=60 << 20),
        name="expert_finish",
    )(every.reshape(planes * count, model_width), hid, own_sum, returned)
    down_grad = down_grad.reshape(share, model_width // 128, local_experts, 128)
    return (token_grad, down_grad.transpose(0, 2, 1, 3).reshape(share, local_experts, model_width))


def solution(mesh):
    placed = (
        P(("expert", "dp"), None),
        P(("expert", "dp"), None),
        P(("expert", "dp"), None),
        P(("expert", "dp"), None),
        P("expert", None, None),
        P("expert", None, None),
        P("expert", None, None),
    )
    return jax.shard_map(
        shards,
        mesh=mesh,
        in_specs=placed,
        out_specs=(P(("expert", "dp"), None), P("dp", "expert", None)),
        check_vma=False,
    )
```
